32 devices in a mesh: groups: 1, tensor: 16 (over z, y, x), sub: 2 (over core).
Axes of the slice: x: 2, y: 2, z: 4, core: 2. Of those that a mesh axis runs over, the one named last changes fastest.
Arguments:
- stored: bfloat16 [8192, 32768], P(('tensor', 'sub')), may hold values from -0.0625 to 0.0625
- tokens: bfloat16 [256, 8192], P(('groups', 'tensor')), may hold values from -6 to 6
- owner_map: int32 [256], replicated, may hold values from 0 to 255, each once
- live_count: int32 [1], P('groups'), may hold values from 128 to 256
Outputs:
- serving_out: bfloat16 [256, 32768], P('groups', ('tensor', 'sub'))
The draws below stay inside these ranges and needn't reach their ends.
Inputs may be any that keep to these rules, and one draw needn't show every extreme that they name: `owner_map`: each of the 256 saved column blocks is named exactly once. Rows from live_count on are padding.
All inputs are finite; a program needn't handle non-finite values.
Results may differ from the reference program's by a relative error of at most 0.001.
Values may be sent and summed in bfloat16 or wider, within the bound.
A program may use at most 128 MiB of HBM per device.

```python
import jax
import jax.numpy as jnp

D = 8192
FF = 32768
BLOCK = 128
TOKENS = 256
NB = 256


def block_levels(rng, extent, cuts, least, top_value):
    factor_of = 1.0
    for axis_at, shards_of in cuts:
        heights = jax.random.uniform(jax.random.fold_in(jax.random.fold_in(rng, 6), axis_at), (shards_of,), jnp.float32, least / len(cuts), top_value / len(cuts))
        factor_of = factor_of * jnp.repeat(jnp.exp(heights), extent[axis_at] // shards_of).reshape((-1,) + (1,) * (len(extent) - 1 - axis_at))
    return factor_of


def noise(key, dims, width, most, cuts=(), kind=jnp.bfloat16):
    factor_of = block_levels(key, dims, cuts, -0.22, 0.18) if cuts else 1.0
    array = jax.random.normal(key, dims, jnp.float32) * width * factor_of
    return jnp.minimum(jnp.maximum(array, -most), most).astype(kind)


def setup_inputs(seed: int = 0, part: int = 0) -> dict:
    seeds = jax.random.split(jax.random.key(seed), 5)
    part_keys = jax.random.split(jax.random.fold_in(seeds[4], part), 5)
    stored = noise(seeds[0], (D, FF), D ** -0.5, 0.0625, ((0, 32),))
    tokens = noise(part_keys[1], (TOKENS, D), 1.0, 6.0, ((0, 16),))
    owner_map = jax.random.permutation(seeds[2], NB).astype(jnp.int32)
    live_count = jax.random.randint(part_keys[3], (1,), TOKENS // 2, TOKENS + 1).astype(jnp.int32)
    return {"stored": stored, "tokens": tokens, "owner_map": owner_map, "live_count": live_count}


def reference(stored, tokens, owner_map, live_count):
    product = jnp.dot(tokens, stored, preferred_element_type=jnp.float32)
    regrouped = jnp.take(product.reshape(TOKENS, NB, BLOCK), owner_map, axis=1).reshape(TOKENS, FF)
    row_ids = jnp.arange(TOKENS, dtype=jnp.int32)
    keep = (row_ids < live_count[0])[:, None]
    return jnp.where(keep, regrouped, jnp.float32(0.0)).astype(jnp.bfloat16)
```

```python
import functools

import jax
import jax.numpy as jnp
from jax import lax
from jax.experimental import pallas as pl
from jax.experimental.pallas import tpu as pltpu
from jax.sharding import PartitionSpec as P

MESH = pl.DeviceIdType.MESH
VMEM_LIMIT = 67043328
TOP = 32767.0
TINY = 1e-33


def portable(stored, tokens, owner_map, live_count):
    row_count = stored.shape[0]
    block_count = owner_map.shape[0]
    width = stored.shape[1] // block_count
    devices = lax.axis_size(("tensor", "sub"))
    per_dev = block_count // devices
    ordered = jnp.take(stored.reshape(row_count, block_count, width), owner_map, axis=1)
    gathered = lax.all_gather(tokens, "tensor", axis=0, tiled=True)
    sectioned = ordered.reshape(row_count, devices, per_dev, width)
    piece = lax.all_to_all(sectioned, ("tensor", "sub"), split_axis=1, concat_axis=0, tiled=True)
    weights = piece.reshape(piece.shape[0], piece.shape[2], piece.shape[3])
    result = jnp.einsum("td,dkc->tkc", gathered, weights, preferred_element_type=jnp.float32)
    product = result.reshape(result.shape[0], per_dev * width)
    row_ids = lax.broadcasted_iota(jnp.int32, (product.shape[0], 1), 0)
    keep = row_ids < live_count[0]
    return jnp.where(keep, product, jnp.float32(0.0)).astype(jnp.bfloat16)


def kernel(T, own_rows, block, parts, map_ref, tok_ref, w_hbm, out_ref, w, tok, *refs):
    t = lax.axis_index("tensor")
    s = lax.axis_index("sub")
    depth = w.shape[1]
    other = 1 - s
    n = len(parts)
    bufs = [refs[7 * i:7 * i + 7] for i in range(n)]
    w_sem, ts, tr, ss, sr, cs, cr, fs, fr = refs[7 * n:]
    rows = bufs[0][2].shape[1]
    bits = [lax.rem(t // 2 ** k, 2) for k in range(4)]
    far = [t + 2 ** k * (1 - 2 * bits[k]) for k in range(4)]
    per_dev = sum(count for count, _ in parts)
    starts = [sum(count for count, _ in parts[:i]) for i in range(n)]

    def load_block(b, carry):
        at = pl.multiple_of(b * block, block)
        pltpu.make_async_copy(w_hbm.at[:, pl.ds(at, block)], w.at[b], w_sem).start()
        return carry

    lax.fori_loop(0, w.shape[0], load_block, 0)

    barrier = pltpu.get_barrier_semaphore()
    for r in range(1, T):
        pl.semaphore_signal(barrier, inc=1, device_id={"tensor": lax.rem(t + r, T), "sub": s}, device_id_type=MESH)
    pl.semaphore_signal(barrier, inc=1, device_id={"tensor": t, "sub": other}, device_id_type=MESH)
    pl.semaphore_wait(barrier, T)

    def token_copy(r):
        to = lax.rem(t + r, T)
        return pltpu.make_async_remote_copy(
            src_ref=tok_ref.at[:, pl.ds(pl.multiple_of(to * 2 * depth, 2 * depth), 2 * depth)],
            dst_ref=tok.at[pl.ds(pl.multiple_of(t * own_rows, own_rows), own_rows), :],
            send_sem=ts.at[r], recv_sem=tr.at[r],
            device_id={"tensor": to, "sub": s}, device_id_type=MESH)

    for r in range(1, T):
        token_copy(r).start()
    tok[pl.ds(pl.multiple_of(t * own_rows, own_rows), own_rows), :] = (
        tok_ref[:, pl.ds(pl.multiple_of(t * 2 * depth, 2 * depth), 2 * depth)])

    def sub_copy(q, j, i):
        stage, wr = bufs[i][:2]
        return pltpu.make_async_remote_copy(
            src_ref=stage.at[j], dst_ref=wr.at[2 * q + j],
            send_sem=ss.at[2 * i + j], recv_sem=sr.at[16 * i + 2 * q + j],
            device_id={"tensor": t, "sub": other}, device_id_type=MESH)

    def place(level, at):
        return (0, 8, 12, 14)[level] + at

    def halving(i, level, at):
        _, _, _, code, unit, code_in, unit_in = bufs[i]
        to = {"tensor": far[parts[i][1][level]], "sub": s}
        here = place(level, at)
        return [
            pltpu.make_async_remote_copy(
                src_ref=unit.at[here], dst_ref=unit_in.at[here], send_sem=fs.at[15 * i + here],
                recv_sem=fr.at[15 * i + here], device_id=to, device_id_type=MESH),
            pltpu.make_async_remote_copy(
                src_ref=code.at[here], dst_ref=code_in.at[here], send_sem=cs.at[15 * i + here],
                recv_sem=cr.at[15 * i + here], device_id=to, device_id_type=MESH),
        ]

    def send(i, level, at, total):
        here = place(level, at)
        most = jnp.maximum(jnp.max(jnp.abs(total), axis=0, keepdims=True), TINY)
        bufs[i][4][here] = most * (1.0 / TOP)
        bufs[i][3][here] = jnp.round(total * (TOP / most)).astype(jnp.int32).astype(jnp.int16)
        for copy in halving(i, level, at):
            copy.start()

    def received(i, level, at):
        for copy in halving(i, level, at):
            copy.wait_recv()
        here = place(level, at)
        return bufs[i][5][here].astype(jnp.int32).astype(jnp.float32) * bufs[i][6][here]

    def first_block(q, j, i, sub):
        g = q // 2
        flips = (1 - lax.rem(q, 2), 1 - j, 1 - g // 2, 1 - lax.rem(g, 2))
        to = 0
        for k, flip in zip(parts[i][1], flips):
            to += lax.rem(bits[k] + flip, 2) * 2 ** k
        return (2 * to + sub) * per_dev + starts[i]

    def columns(base, m):
        return w[map_ref[base + m]]

    def fill(q, j, i):
        base = first_block(q, j, i, other)
        for m in range(parts[i][0]):
            bufs[i][0][j, :, m * block:(m + 1) * block] = columns(base, m)
        sub_copy(q, j, i).start()

    pltpu.make_async_copy(w, w, w_sem).wait()
    for j in range(2):
        for i in range(n):
            fill(0, j, i)
    for r in range(1, T):
        token_copy(r).wait()

    def compute(q, carry):
        kept, g = lax.rem(q, 2), q // 2
        mine = tok[0:rows, pl.ds(pl.multiple_of(s * depth, depth), depth)]
        theirs = tok[0:rows, pl.ds(pl.multiple_of(other * depth, depth), depth)]
        for j in range(2):
            for i in range(n):
                base = first_block(q, j, i, s)
                own = jnp.concatenate([columns(base, m) for m in range(parts[i][0])], axis=1)
                total = jnp.dot(mine, own, preferred_element_type=jnp.float32)
                sub_copy(q, j, i).wait()
                total += jnp.dot(theirs, bufs[i][1][2 * q + j], preferred_element_type=jnp.float32)

                @pl.when(kept == 0)
                def _():
                    send(i, 0, 2 * g + j, total)

                @pl.when(kept == 1)
                def _():
                    bufs[i][2][2 * g + j] = total

                @pl.when(q < 7)
                def _():
                    fill(q + 1, j, i)
        return carry

    def finish(g):
        for i in range(n):
            bufs[i][2][2 * g + 1] += received(i, 1, g)

    def step(at, carry):
        g = at - 2

        @pl.when(g >= 0)
        def _():
            for i in range(n):
                send(i, 1, g, bufs[i][2][2 * g] + received(i, 0, 2 * g))

            for i in range(n):
                bufs[i][2][2 * g + 1] += received(i, 0, 2 * g + 1)

        lax.fori_loop(jnp.maximum(2 * g + 3, 0), jnp.minimum(2 * g + 5, 8), compute, 0)

        @pl.when(g >= 1)
        def _():
            finish(g - 1)

            @pl.when(g < 3)
            def _():
                for i in range(n):
                    send(i, 2, g - 1, bufs[i][2][2 * g - 1])

            @pl.when(g == 3)
            def _():
                for i in range(n):
                    send(i, 3, 0, bufs[i][2][5] + received(i, 2, 0))
        return carry

    lax.fori_loop(0, 6, step, 0)
    for i in range(n):
        total = bufs[i][2][7] + received(i, 2, 1)
        total += received(i, 1, 3)
        total += received(i, 3, 0)
        out_ref[0:rows, starts[i] * block:(starts[i] + parts[i][0]) * block] = total.astype(out_ref.dtype)
    for i in range(n):
        for level in range(4):
            for at in range(8 >> level):
                for copy in halving(i, level, at):
                    copy.wait_send()


def split(per_dev):
    last = per_dev // 4
    rest = per_dev - last
    return (((rest + 1) // 2, (0, 1, 2, 3)), (rest // 2, (1, 0, 2, 3)), (last, (2, 3, 0, 1)))


def plan(depth, n_blocks, own_rows, block, T, parts, live):
    sems = pltpu.SemaphoreType.DMA
    f32, bf16 = jnp.float32, jnp.bfloat16
    n = len(parts)
    shapes = [pltpu.VMEM((n_blocks, depth, block), bf16), pltpu.VMEM((own_rows * T, 2 * depth), bf16)]
    for count, _ in parts:
        wide = count * block
        shapes += [pltpu.VMEM((2, depth, wide), bf16), pltpu.VMEM((16, depth, wide), bf16)]
        shapes += [pltpu.VMEM((8, live, wide), f32)]
        shapes += [pltpu.VMEM((15, live, wide), jnp.int16), pltpu.VMEM((15, 1, wide), f32)] * 2
    counts = ((), (T,), (T,), (2 * n,), (16 * n,)) + ((15 * n,),) * 4
    return shapes + [sems(k) for k in counts]


def fits(depth, ff, own_rows, T, subs, n_blocks):
    if T.bit_length() != 5 or T & (T - 1) or subs != 2 or n_blocks % (8 * T):
        return False
    rows, wide = own_rows * T, ff // (2 * T)
    used = 2 * (depth * ff + rows * 2 * depth + 18 * depth * wide) + (4 * 8 + 2 * 30) * rows * wide
    return used + (4 << 20) < VMEM_LIMIT


def on_device(stored, tokens, owner_map, live_count):
    depth, ff = stored.shape
    own_rows = tokens.shape[0]
    n_blocks = owner_map.shape[0]
    block = ff // n_blocks
    T, subs = lax.axis_size("tensor"), lax.axis_size("sub")
    if not fits(depth, ff, own_rows, T, subs, n_blocks):
        return portable(stored, tokens, owner_map, live_count)
    rows = own_rows * T
    parts = split(n_blocks // (2 * T))
    unit = max(rows // 8, 16)
    sizes = [n for n in range(rows - 4 * unit, rows, unit) if n > 0] + [rows]

    def call(n, which):
        return pl.pallas_call(
            functools.partial(kernel, T, own_rows, block, parts),
            out_shape=jax.ShapeDtypeStruct((rows, ff // (2 * T)), jnp.bfloat16),
            in_specs=[pl.BlockSpec(memory_space=pltpu.SMEM), pl.BlockSpec(memory_space=pltpu.VMEM),
                      pl.BlockSpec(memory_space=pl.ANY)],
            out_specs=pl.BlockSpec(memory_space=pltpu.VMEM),
            scratch_shapes=plan(depth, n_blocks, own_rows, block, T, parts, n),
            compiler_params=pltpu.CompilerParams(
                collective_id=which, has_side_effects=True, vmem_limit_bytes=VMEM_LIMIT),
        )

    most = live_count[0]
    if lax.axis_size("groups") > 1:
        most = lax.pmax(most, "groups")
    which = sum((most > n).astype(jnp.int32) for n in sizes[:-1])
    product = lax.switch(which, [call(n, i) for i, n in enumerate(sizes)], owner_map, tokens, stored)
    keep = lax.broadcasted_iota(jnp.int32, (rows, 1), 0) < live_count[0]
    return jnp.where(keep, product, jnp.bfloat16(0.0))


def solution(mesh):
    placed = (P(("tensor", "sub"), None), P(("groups", "tensor"), None), P(), P("groups"))
    return jax.shard_map(
        on_device,
        mesh=mesh,
        in_specs=placed,
        out_specs=P("groups", ("tensor", "sub")),
        check_vma=False,
    )
```

```python
import functools

import jax
import jax.numpy as jnp
from jax import lax
from jax.experimental import pallas as pl
from jax.experimental.pallas import tpu as pltpu
from jax.sharding import PartitionSpec as P

MESH = pl.DeviceIdType.MESH
VMEM_LIMIT = 67043328
TOP = 32767.0
TINY = 1e-33
AHEAD = 4
LOADS = 8
HALVING = ((2, 0, 1, 3), (0, 2, 1, 3), (1, 0, 2, 3), (1, 0, 2, 3))
ORDER = (
    15, 31, 47, 14, 30, 63, 13, 29, 46, 7, 23, 39, 62, 6, 22, 55, 45, 5, 21, 38, 61, 12, 54, 44, 11, 37, 60, 10, 53, 43, 4, 9,
    36, 59, 3, 8, 52, 2, 35, 51, 42, 1, 58, 41, 28, 34, 57, 27, 50, 40, 26, 33, 56, 0, 20, 49, 25, 19, 24, 18, 32, 17, 48, 16)
PLACE = (0, 8, 12, 14)


def portable(stored, tokens, owner_map, live_count):
    row_count = stored.shape[0]
    block_count = owner_map.shape[0]
    width = stored.shape[1] // block_count
    devices = lax.axis_size(("tensor", "sub"))
    per_dev = block_count // devices
    ordered = jnp.take(stored.reshape(row_count, block_count, width), owner_map, axis=1)
    gathered = lax.all_gather(tokens, "tensor", axis=0, tiled=True)
    sectioned = ordered.reshape(row_count, devices, per_dev, width)
    piece = lax.all_to_all(sectioned, ("tensor", "sub"), split_axis=1, concat_axis=0, tiled=True)
    weights = piece.reshape(piece.shape[0], piece.shape[2], piece.shape[3])
    result = jnp.einsum("td,dkc->tkc", gathered, weights, preferred_element_type=jnp.float32)
    product = result.reshape(result.shape[0], per_dev * width)
    row_ids = lax.broadcasted_iota(jnp.int32, (product.shape[0], 1), 0)
    keep = row_ids < live_count[0]
    return jnp.where(keep, product, jnp.float32(0.0)).astype(jnp.bfloat16)


def pick(values, at):
    out = values[-1]
    for k in range(len(values) - 2, -1, -1):
        out = jnp.where(at == k, values[k], out)
    return out


def lookup(at):
    words = [sum(v << (6 * k) for k, v in enumerate(ORDER[j:j + 5])) for j in range(0, len(ORDER), 5)]
    word = pick([jnp.int32(v) for v in words], lax.div(at, 5))
    return lax.rem(lax.div(word, pick([jnp.int32(64 ** k) for k in range(5)], lax.rem(at, 5))), 64)


def kernel(T, own_rows, block, map_ref, tok_ref, w_hbm, out_ref, w, tok, stage, wr, code, unit, code_in, unit_in,
           w_sem, ts, tr, ss, sr, cs, cr, fs, fr):
    t = lax.axis_index("tensor")
    s = lax.axis_index("sub")
    other = 1 - s
    depth = w.shape[0]
    rows, wide = code.shape[1:]
    blocks = wide // block
    per_dev = len(HALVING) * blocks
    steps = len(ORDER)
    bits = [lax.rem(t // 2 ** k, 2) for k in range(4)]
    far = [t + 2 ** k * (1 - 2 * bits[k]) for k in range(4)]

    span = depth // LOADS
    for c in range(LOADS):
        pltpu.make_async_copy(w_hbm.at[pl.ds(c * span, span), :], w.at[pl.ds(c * span, span), :], w_sem).start()

    barrier = pltpu.get_barrier_semaphore()
    for r in range(1, T):
        pl.semaphore_signal(barrier, inc=1, device_id={"tensor": lax.rem(t + r, T), "sub": s}, device_id_type=MESH)
    pl.semaphore_signal(barrier, inc=1, device_id={"tensor": t, "sub": other}, device_id_type=MESH)
    pl.semaphore_wait(barrier, T)

    def token_copy(r):
        to = lax.rem(t + r, T)
        return pltpu.make_async_remote_copy(
            src_ref=tok_ref.at[:, pl.ds(pl.multiple_of(to * 2 * depth, 2 * depth), 2 * depth)],
            dst_ref=tok.at[pl.ds(pl.multiple_of(t * own_rows, own_rows), own_rows), :],
            send_sem=ts.at[r], recv_sem=tr.at[r],
            device_id={"tensor": to, "sub": s}, device_id_type=MESH)

    for r in range(1, T):
        token_copy(r).start()
    tok[pl.ds(pl.multiple_of(t * own_rows, own_rows), own_rows), :] = (
        tok_ref[:, pl.ds(pl.multiple_of(t * 2 * depth, 2 * depth), 2 * depth)])

    def sub_copy(k):
        slot = lax.rem(k, AHEAD)
        return pltpu.make_async_remote_copy(
            src_ref=stage.at[slot], dst_ref=wr.at[k], send_sem=ss.at[slot], recv_sem=sr.at[k],
            device_id={"tensor": t, "sub": other}, device_id_type=MESH)

    def halving(part, level, place):
        here = 15 * part + place
        to = {"tensor": pick([far[order[level]] for order in HALVING], part), "sub": s}
        return [
            pltpu.make_async_remote_copy(
                src_ref=unit.at[here], dst_ref=unit_in.at[here], send_sem=fs.at[here],
                recv_sem=fr.at[here], device_id=to, device_id_type=MESH),
            pltpu.make_async_remote_copy(
                src_ref=code.at[here], dst_ref=code_in.at[here], send_sem=cs.at[here],
                recv_sem=cr.at[here], device_id=to, device_id_type=MESH),
        ]

    def first_block(step, sub):
        part, flips = lax.div(step, 16), lax.rem(step, 16)
        flip = [lax.rem(lax.div(flips, 2 ** (3 - k)), 2) for k in range(4)]
        to = [sum(lax.rem(bits[order[k]] + flip[k], 2) * 2 ** order[k] for k in range(4)) for order in HALVING]
        return (2 * pick(to, part) + sub) * per_dev + part * blocks

    def columns(base, m):
        return w[:, pl.ds(map_ref[base + m] * block, block)]

    def fill(k):
        base = first_block(lookup(k), other)
        slot = lax.rem(k, AHEAD)
        for m in range(blocks):
            stage[slot, :, m * block:(m + 1) * block] = columns(base, m)
        sub_copy(k).start()

    pltpu.make_async_copy(w, w, w_sem).wait()
    for k in range(AHEAD):
        fill(k)
    for r in range(1, T):
        token_copy(r).wait()

    def run(k, carry):
        step = lookup(k)
        part, flips = lax.div(step, 16), lax.rem(step, 16)
        base = first_block(step, s)
        sub_copy(k).wait()

        def partial():
            own = jnp.concatenate([columns(base, m) for m in range(blocks)], axis=1)
            mine = tok[0:rows, pl.ds(pl.multiple_of(s * depth, depth), depth)]
            theirs = tok[0:rows, pl.ds(pl.multiple_of(other * depth, depth), depth)]
            total = jnp.dot(mine, own, preferred_element_type=jnp.float32)
            return total + jnp.dot(theirs, wr[k], preferred_element_type=jnp.float32)

        for level in range(5):
            least = (8 >> level) if level < 4 else 0

            @pl.when((flips >= least) & (flips < max(2 * least, 1)))
            def _():
                total = partial()
                for before in range(level):
                    place = PLACE[before] + flips
                    for copy in halving(part, before, place):
                        copy.wait_recv()
                    here = 15 * part + place
                    total += code_in[here].astype(jnp.int32).astype(jnp.float32) * unit_in[here]
                if level == 4:
                    out_ref[0:rows, pl.ds(pl.multiple_of(part * wide, wide), wide)] = total.astype(out_ref.dtype)
                    return
                place = PLACE[level] + flips - least
                here = 15 * part + place
                most = jnp.maximum(jnp.max(jnp.abs(total), axis=0, keepdims=True), TINY)
                unit[here] = most * (1.0 / TOP)
                code[here] = jnp.round(total * (TOP / most)).astype(jnp.int32).astype(jnp.int16)
                for copy in halving(part, level, place):
                    copy.start()

        @pl.when(k < steps - AHEAD)
        def _():
            fill(k + AHEAD)
        return carry

    lax.fori_loop(0, steps, run, 0)

    def drain(here, carry):
        part, place = lax.div(here, 15), lax.rem(here, 15)
        for copy in halving(part, 0, place):
            copy.wait_send()
        return carry

    lax.fori_loop(0, 15 * len(HALVING), drain, 0)


def plan(depth, ff, own_rows, block, T, live):
    sems = pltpu.SemaphoreType.DMA
    f32, bf16 = jnp.float32, jnp.bfloat16
    n = len(HALVING)
    wide = ff // (2 * T * n)
    shapes = [pltpu.VMEM((depth, ff), bf16), pltpu.VMEM((own_rows * T, 2 * depth), bf16)]
    shapes += [pltpu.VMEM((AHEAD, depth, wide), bf16), pltpu.VMEM((16 * n, depth, wide), bf16)]
    shapes += [pltpu.VMEM((15 * n, live, wide), jnp.int16), pltpu.VMEM((15 * n, 1, wide), f32)] * 2
    counts = ((), (T,), (T,), (AHEAD,), (16 * n,)) + ((15 * n,),) * 4
    return shapes + [sems(k) for k in counts]


def fits(depth, ff, own_rows, T, subs, n_blocks):
    n = len(HALVING)
    if T.bit_length() != 5 or T & (T - 1) or subs != 2 or n_blocks % (2 * T * n) or depth % (16 * LOADS) or own_rows % 16:
        return False
    rows, wide = own_rows * T, ff // (2 * T * n)
    used = 2 * (depth * ff + 2 * rows * 2 * depth + (AHEAD + 16 * n) * depth * wide + 60 * n * rows * wide)
    return used + 4 * rows * n * wide + (4 << 20) < VMEM_LIMIT


def on_device(stored, tokens, owner_map, live_count):
    depth, ff = stored.shape
    own_rows = tokens.shape[0]
    n_blocks = owner_map.shape[0]
    block = ff // n_blocks
    T, subs = lax.axis_size("tensor"), lax.axis_size("sub")
    if not fits(depth, ff, own_rows, T, subs, n_blocks):
        return portable(stored, tokens, owner_map, live_count)
    rows = own_rows * T
    unit = max(rows // 16, 16)
    sizes = [n for n in range(rows // 2, rows, unit)] + [rows]

    def call(n, which):
        return pl.pallas_call(
            functools.partial(kernel, T, own_rows, block),
            out_shape=jax.ShapeDtypeStruct((rows, ff // (2 * T)), jnp.bfloat16),
            in_specs=[pl.BlockSpec(memory_space=pltpu.SMEM), pl.BlockSpec(memory_space=pltpu.VMEM),
                      pl.BlockSpec(memory_space=pl.ANY)],
            out_specs=pl.BlockSpec(memory_space=pltpu.VMEM),
            scratch_shapes=plan(depth, ff, own_rows, block, T, n),
            compiler_params=pltpu.CompilerParams(
                collective_id=which, has_side_effects=True, vmem_limit_bytes=VMEM_LIMIT),
        )

    most = live_count[0]
    if lax.axis_size("groups") > 1:
        most = lax.pmax(most, "groups")
    which = sum((most > n).astype(jnp.int32) for n in sizes[:-1])
    product = lax.switch(which, [call(n, i) for i, n in enumerate(sizes)], owner_map, tokens, stored)
    keep = lax.broadcasted_iota(jnp.int32, product.shape, 0) < live_count[0]
    return jnp.where(keep, product, jnp.bfloat16(0.0))


def solution(mesh):
    placed = (P(("tensor", "sub"), None), P(("groups", "tensor"), None), P(), P("groups"))
    return jax.shard_map(
        on_device,
        mesh=mesh,
        in_specs=placed,
        out_specs=P("groups", ("tensor", "sub")),
        check_vma=False,
    )
```

```python
import functools

import jax
import jax.numpy as jnp
from jax import lax
from jax.experimental import pallas as pl
from jax.experimental.pallas import tpu as pltpu
from jax.sharding import PartitionSpec as P

MESH = pl.DeviceIdType.MESH
VMEM_LIMIT = 67043328
TOP = 32767.0
TINY = 1e-33
AHEAD = 4
LOADS = 8
HALVING = ((2, 0, 1, 3), (0, 2, 1, 3), (1, 0, 2, 3), (1, 0, 2, 3))
ORDER = (
    61, 29, 15, 63, 11, 31, 26, 46, 14, 8, 44, 30, 42, 27, 13, 45, 47, 38, 25, 23, 7, 12, 55, 22, 21, 9, 59, 19, 57, 5,
    10, 3, 53, 43, 39, 17, 62, 51, 58, 28, 1, 4, 37, 41, 6, 35, 60, 18, 49, 54, 24, 34, 40, 36, 33, 2, 20, 56, 52, 50, 0,
    16, 32, 48)
PLACE = (0, 8, 12, 14)


def portable(stored, tokens, owner_map, live_count):
    row_count = stored.shape[0]
    block_count = owner_map.shape[0]
    width = stored.shape[1] // block_count
    devices = lax.axis_size(("tensor", "sub"))
    per_dev = block_count // devices
    ordered = jnp.take(stored.reshape(row_count, block_count, width), owner_map, axis=1)
    gathered = lax.all_gather(tokens, "tensor", axis=0, tiled=True)
    sectioned = ordered.reshape(row_count, devices, per_dev, width)
    piece = lax.all_to_all(sectioned, ("tensor", "sub"), split_axis=1, concat_axis=0, tiled=True)
    weights = piece.reshape(piece.shape[0], piece.shape[2], piece.shape[3])
    result = jnp.einsum("td,dkc->tkc", gathered, weights, preferred_element_type=jnp.float32)
    product = result.reshape(result.shape[0], per_dev * width)
    row_ids = lax.broadcasted_iota(jnp.int32, (product.shape[0], 1), 0)
    keep = row_ids < live_count[0]
    return jnp.where(keep, product, jnp.float32(0.0)).astype(jnp.bfloat16)


def pick(values, at):
    if len(values) == 1:
        return values[0]
    half = len(values) // 2
    return jnp.where(at < half, pick(values[:half], at), pick(values[half:], at - half))


def lookup(k):
    words = [sum(v << (6 * j) for j, v in enumerate(ORDER[at:at + 4])) for at in range(0, len(ORDER), 4)]
    word = pick([jnp.int32(v) for v in words], lax.div(k, 4))
    return lax.rem(pick([lax.div(word, 64 ** j) for j in range(4)], lax.rem(k, 4)), 64)


def kernel(T, own_rows, block, map_ref, tok_ref, w_hbm, out_ref, w, tok, stage, wr, code, unit, code_in, unit_in, out,
           own_ids, other_ids, w_sem, out_sem, ts, tr, ss, sr, cs, cr, fs, fr):
    t = lax.axis_index("tensor")
    s = lax.axis_index("sub")
    other = 1 - s
    depth = w.shape[0]
    rows, wide = code.shape[1:]
    blocks = wide // block
    per_dev = len(HALVING) * blocks
    steps = len(ORDER)
    bits = [lax.rem(t // 2 ** k, 2) for k in range(4)]
    far = [t + 2 ** k * (1 - 2 * bits[k]) for k in range(4)]

    span = depth // LOADS
    for c in range(LOADS):
        pltpu.make_async_copy(w_hbm.at[pl.ds(c * span, span), :], w.at[pl.ds(c * span, span), :], w_sem).start()

    barrier = pltpu.get_barrier_semaphore()
    for r in range(1, T):
        pl.semaphore_signal(barrier, inc=1, device_id={"tensor": lax.rem(t + r, T), "sub": s}, device_id_type=MESH)
    pl.semaphore_signal(barrier, inc=1, device_id={"tensor": t, "sub": other}, device_id_type=MESH)
    pl.semaphore_wait(barrier, T)

    def token_copy(r):
        to = lax.rem(t + r, T)
        return pltpu.make_async_remote_copy(
            src_ref=tok_ref.at[:, pl.ds(pl.multiple_of(to * 2 * depth, 2 * depth), 2 * depth)],
            dst_ref=tok.at[pl.ds(pl.multiple_of(t * own_rows, own_rows), own_rows), :],
            send_sem=ts.at[r], recv_sem=tr.at[r],
            device_id={"tensor": to, "sub": s}, device_id_type=MESH)

    for r in range(1, T):
        token_copy(r).start()
    tok[pl.ds(pl.multiple_of(t * own_rows, own_rows), own_rows), :] = (
        tok_ref[:, pl.ds(pl.multiple_of(t * 2 * depth, 2 * depth), 2 * depth)])

    def sub_copy(k):
        slot = lax.rem(k, AHEAD)
        return pltpu.make_async_remote_copy(
            src_ref=stage.at[slot], dst_ref=wr.at[k], send_sem=ss.at[slot], recv_sem=sr.at[k],
            device_id={"tensor": t, "sub": other}, device_id_type=MESH)

    def halving(part, level, place):
        here = 15 * part + place
        to = {"tensor": pick([far[order[level]] for order in HALVING], part), "sub": s}
        return [
            pltpu.make_async_remote_copy(
                src_ref=unit.at[here], dst_ref=unit_in.at[here], send_sem=fs.at[here],
                recv_sem=fr.at[here], device_id=to, device_id_type=MESH),
            pltpu.make_async_remote_copy(
                src_ref=code.at[here], dst_ref=code_in.at[here], send_sem=cs.at[here],
                recv_sem=cr.at[here], device_id=to, device_id_type=MESH),
        ]

    moved = [0]
    for k in range(4):
        moved += [m + (far[k] - t) for m in moved]
    for k, step in enumerate(ORDER):
        part, flips = step // 16, step % 16
        which = sum(2 ** HALVING[part][j] for j in range(4) if flips >> (3 - j) & 1)
        for ids, sub in ((own_ids, s), (other_ids, other)):
            base = (2 * (t + moved[which]) + sub) * per_dev + part * blocks
            for m in range(blocks):
                ids[k * blocks + m] = map_ref[base + m]

    def columns(ids, k, m):
        return w[:, pl.ds(ids[k * blocks + m] * block, block)]

    def fill(k, at):
        for m in range(blocks):
            stage[lax.rem(k, AHEAD), :, m * block:(m + 1) * block] = columns(other_ids, at, m)

    pltpu.make_async_copy(w, w, w_sem).wait()
    for k in range(AHEAD):
        fill(k, k)
        sub_copy(k).start()
    for r in range(1, T):
        token_copy(r).wait()

    def out_copy(part):
        return pltpu.make_async_copy(
            out.at[part], out_ref.at[0:rows, pl.ds(pl.multiple_of(part * wide, wide), wide)], out_sem.at[part])

    def run(k, carry):
        step = lookup(k)
        part, flips = lax.div(step, 16), lax.rem(step, 16)
        sub_copy(k).wait()
        fill(k, jnp.minimum(k + AHEAD, steps - 1))

        @pl.when(k < steps - AHEAD)
        def _():
            sub_copy(k + AHEAD).start()

        def partial():
            own = jnp.concatenate([columns(own_ids, k, m) for m in range(blocks)], axis=1)
            mine = tok[0:rows, pl.ds(pl.multiple_of(s * depth, depth), depth)]
            theirs = tok[0:rows, pl.ds(pl.multiple_of(other * depth, depth), depth)]
            total = jnp.dot(mine, own, preferred_element_type=jnp.float32)
            return total + jnp.dot(theirs, wr[k], preferred_element_type=jnp.float32)

        for level in range(5):
            least = (8 >> level) if level < 4 else 0

            @pl.when((flips >= least) & (flips < max(2 * least, 1)))
            def _():
                total = partial()
                for before in range(level):
                    place = PLACE[before] + flips
                    for copy in halving(part, before, place):
                        copy.wait_recv()
                    here = 15 * part + place
                    total += code_in[here].astype(jnp.int32).astype(jnp.float32) * unit_in[here]
                if level == 4:
                    out[part] = total.astype(out.dtype)
                    out_copy(part).start()
                    return
                place = PLACE[level] + flips - least
                here = 15 * part + place
                most = jnp.maximum(jnp.max(jnp.abs(total), axis=0, keepdims=True), TINY)
                unit[here] = most * (1.0 / TOP)
                code[here] = jnp.round(total * (TOP / most)).astype(jnp.int32).astype(jnp.int16)
                for copy in halving(part, level, place):
                    copy.start()
        return carry

    lax.fori_loop(0, steps, run, 0)

    def drain(here, carry):
        part, place = lax.div(here, 15), lax.rem(here, 15)
        for copy in halving(part, 0, place):
            copy.wait_send()
        return carry

    lax.fori_loop(0, 15 * len(HALVING), drain, 0)
    for part in range(len(HALVING)):
        out_copy(part).wait()


def plan(depth, ff, own_rows, block, T, live):
    sems = pltpu.SemaphoreType.DMA
    f32, bf16 = jnp.float32, jnp.bfloat16
    n = len(HALVING)
    wide = ff // (2 * T * n)
    shapes = [pltpu.VMEM((depth, ff), bf16), pltpu.VMEM((own_rows * T, 2 * depth), bf16)]
    shapes += [pltpu.VMEM((AHEAD, depth, wide), bf16), pltpu.VMEM((16 * n, depth, wide), bf16)]
    shapes += [pltpu.VMEM((15 * n, live, wide), jnp.int16), pltpu.VMEM((15 * n, 1, wide), f32)] * 2
    shapes += [pltpu.VMEM((n, live, wide), bf16)] + [pltpu.SMEM((16 * n * (wide // block),), jnp.int32)] * 2
    counts = ((), (n,), (T,), (T,), (AHEAD,), (16 * n,)) + ((15 * n,),) * 4
    return shapes + [sems(k) for k in counts]


def fits(depth, ff, own_rows, T, subs, n_blocks):
    n = len(HALVING)
    if T.bit_length() != 5 or T & (T - 1) or subs != 2 or n_blocks % (2 * T * n) or depth % (16 * LOADS) or own_rows % 16:
        return False
    rows, wide = own_rows * T, ff // (2 * T * n)
    used = 2 * (depth * ff + 2 * rows * 2 * depth + (AHEAD + 16 * n) * depth * wide + 60 * n * rows * wide)
    return used + 4 * rows * n * wide + (4 << 20) < VMEM_LIMIT


def on_device(stored, tokens, owner_map, live_count):
    depth, ff = stored.shape
    own_rows = tokens.shape[0]
    n_blocks = owner_map.shape[0]
    block = ff // n_blocks
    T, subs = lax.axis_size("tensor"), lax.axis_size("sub")
    if not fits(depth, ff, own_rows, T, subs, n_blocks):
        return portable(stored, tokens, owner_map, live_count)
    rows = own_rows * T
    unit = max(rows // 16, 16)
    sizes = [n for n in range(rows // 2, rows, unit)] + [rows]

    def call(n, which):
        return pl.pallas_call(
            functools.partial(kernel, T, own_rows, block),
            out_shape=jax.ShapeDtypeStruct((rows, ff // (2 * T)), jnp.bfloat16),
            in_specs=[pl.BlockSpec(memory_space=pltpu.SMEM), pl.BlockSpec(memory_space=pltpu.VMEM),
                      pl.BlockSpec(memory_space=pl.ANY)],
            out_specs=pl.BlockSpec(memory_space=pl.ANY),
            scratch_shapes=plan(depth, ff, own_rows, block, T, n),
            compiler_params=pltpu.CompilerParams(
                collective_id=which, has_side_effects=True, vmem_limit_bytes=VMEM_LIMIT),
        )

    most = live_count[0]
    if lax.axis_size("groups") > 1:
        most = lax.pmax(most, "groups")
    which = sum((most > n).astype(jnp.int32) for n in sizes[:-1])
    product = lax.switch(which, [call(n, i) for i, n in enumerate(sizes)], owner_map, tokens, stored)
    keep = lax.broadcasted_iota(jnp.int32, product.shape, 0) < live_count[0]
    return jnp.where(keep, product, jnp.bfloat16(0.0))


def solution(mesh):
    placed = (P(("tensor", "sub"), None), P(("groups", "tensor"), None), P(), P("groups"))
    return jax.shard_map(
        on_device,
        mesh=mesh,
        in_specs=placed,
        out_specs=P("groups", ("tensor", "sub")),
        check_vma=False,
    )
```

```python
import functools

import jax
import jax.numpy as jnp
from jax import lax
from jax.experimental import pallas as pl
from jax.experimental.pallas import tpu as pltpu
from jax.sharding import PartitionSpec as P

MESH = pl.DeviceIdType.MESH
VMEM_LIMIT = 60 << 20
TOP = 32767.0
TINY = 1e-33
AHEAD = 4
LOADS = 8
HALVING = ((2, 0, 1, 3), (0, 2, 1, 3), (1, 0, 2, 3), (1, 0, 2, 3))
ORDER = (
    61, 29, 15, 63, 11, 31, 26, 46, 14, 8, 44, 30, 42, 27, 13, 45, 47, 38, 25, 23, 7, 12, 55, 22, 21, 9, 59, 19, 57, 5,
    10, 3, 53, 43, 39, 17, 62, 51, 58, 28, 1, 4, 37, 41, 6, 35, 60, 18, 49, 54, 24, 34, 40, 36, 33, 2, 20, 56, 52, 50, 0,
    16, 32, 48)
PLACE = (0, 8, 12, 14)


def portable(stored, tokens, owner_map, live_count):
    row_count = stored.shape[0]
    block_count = owner_map.shape[0]
    width = stored.shape[1] // block_count
    devices = lax.axis_size(("tensor", "sub"))
    per_dev = block_count // devices
    ordered = jnp.take(stored.reshape(row_count, block_count, width), owner_map, axis=1)
    gathered = lax.all_gather(tokens, "tensor", axis=0, tiled=True)
    sectioned = ordered.reshape(row_count, devices, per_dev, width)
    piece = lax.all_to_all(sectioned, ("tensor", "sub"), split_axis=1, concat_axis=0, tiled=True)
    weights = piece.reshape(piece.shape[0], piece.shape[2], piece.shape[3])
    result = jnp.einsum("td,dkc->tkc", gathered, weights, preferred_element_type=jnp.float32)
    product = result.reshape(result.shape[0], per_dev * width)
    row_ids = lax.broadcasted_iota(jnp.int32, (product.shape[0], 1), 0)
    keep = row_ids < live_count[0]
    return jnp.where(keep, product, jnp.float32(0.0)).astype(jnp.bfloat16)


def pick(values, at):
    if len(values) == 1:
        return values[0]
    half = len(values) // 2
    return jnp.where(at < half, pick(values[:half], at), pick(values[half:], at - half))


def lookup(k):
    words = [sum(v << (6 * j) for j, v in enumerate(ORDER[at:at + 4])) for at in range(0, len(ORDER), 4)]
    word = pick([jnp.int32(v) for v in words], lax.div(k, 4))
    return lax.rem(pick([lax.div(word, 64 ** j) for j in range(4)], lax.rem(k, 4)), 64)


def kernel(T, own_rows, block, map_hbm, tok_hbm, w_hbm, out_ref, map_ref, tok_ref, w, tok, stage, wr, code, unit, code_in, unit_in,
           own_ids, other_ids, map_sem, tok_sem, w_sem, ts, tr, ss, sr, cs, cr, fs, fr):
    t = lax.axis_index("tensor")
    s = lax.axis_index("sub")
    other = 1 - s
    depth = w.shape[0]
    rows, wide = code.shape[1:]
    blocks = wide // block
    per_dev = len(HALVING) * blocks
    steps = len(ORDER)
    bits = [lax.rem(t // 2 ** k, 2) for k in range(4)]
    far = [t + 2 ** k * (1 - 2 * bits[k]) for k in range(4)]

    barrier = pltpu.get_barrier_semaphore()
    for r in range(1, T):
        pl.semaphore_signal(barrier, inc=1, device_id={"tensor": lax.rem(t + r, T), "sub": s}, device_id_type=MESH)
    pl.semaphore_signal(barrier, inc=1, device_id={"tensor": t, "sub": other}, device_id_type=MESH)
    map_copy = pltpu.make_async_copy(map_hbm, map_ref, map_sem)
    map_copy.start()
    own_copy = pltpu.make_async_copy(tok_hbm, tok_ref, tok_sem)
    own_copy.start()
    own_copy.wait()
    span = depth // LOADS
    for c in range(LOADS):
        pltpu.make_async_copy(w_hbm.at[pl.ds(c * span, span), :], w.at[pl.ds(c * span, span), :], w_sem).start()
    pl.semaphore_wait(barrier, T)

    def token_copy(r):
        to = lax.rem(t + r, T)
        return pltpu.make_async_remote_copy(
            src_ref=tok_ref.at[:, pl.ds(pl.multiple_of(to * 2 * depth, 2 * depth), 2 * depth)],
            dst_ref=tok.at[pl.ds(pl.multiple_of(t * own_rows, own_rows), own_rows), :],
            send_sem=ts.at[r], recv_sem=tr.at[r],
            device_id={"tensor": to, "sub": s}, device_id_type=MESH)

    for r in range(1, T):
        token_copy(r).start()
    tok[pl.ds(pl.multiple_of(t * own_rows, own_rows), own_rows), :] = (
        tok_ref[:, pl.ds(pl.multiple_of(t * 2 * depth, 2 * depth), 2 * depth)])

    def sub_copy(k):
        slot = lax.rem(k, AHEAD)
        return pltpu.make_async_remote_copy(
            src_ref=stage.at[slot], dst_ref=wr.at[k], send_sem=ss.at[slot], recv_sem=sr.at[k],
            device_id={"tensor": t, "sub": other}, device_id_type=MESH)

    def halving(part, level, place):
        here = 15 * part + place
        to = {"tensor": pick([far[order[level]] for order in HALVING], part), "sub": s}
        return [
            pltpu.make_async_remote_copy(
                src_ref=unit.at[here], dst_ref=unit_in.at[here], send_sem=fs.at[here],
                recv_sem=fr.at[here], device_id=to, device_id_type=MESH),
            pltpu.make_async_remote_copy(
                src_ref=code.at[here], dst_ref=code_in.at[here], send_sem=cs.at[here],
                recv_sem=cr.at[here], device_id=to, device_id_type=MESH),
        ]

    map_copy.wait()
    moved = [0]
    for k in range(4):
        moved += [m + (far[k] - t) for m in moved]
    for k, step in enumerate(ORDER):
        part, flips = step // 16, step % 16
        which = sum(2 ** HALVING[part][j] for j in range(4) if flips >> (3 - j) & 1)
        for ids, sub in ((own_ids, s), (other_ids, other)):
            base = (2 * (t + moved[which]) + sub) * per_dev + part * blocks
            for m in range(blocks):
                ids[k * blocks + m] = map_ref[base + m]

    def columns(ids, k, m):
        return w[:, pl.ds(ids[k * blocks + m] * block, block)]

    def fill(k, at):
        for m in range(blocks):
            stage[lax.rem(k, AHEAD), :, m * block:(m + 1) * block] = columns(other_ids, at, m)

    pltpu.make_async_copy(w, w, w_sem).wait()
    for k in range(AHEAD):
        fill(k, k)
        sub_copy(k).start()
    for r in range(1, T):
        token_copy(r).wait()

    def run(k, carry):
        step = lookup(k)
        part, flips = lax.div(step, 16), lax.rem(step, 16)
        sub_copy(k).wait()
        fill(k, jnp.minimum(k + AHEAD, steps - 1))

        @pl.when(k < steps - AHEAD)
        def _():
            sub_copy(k + AHEAD).start()

        def partial():
            own = jnp.concatenate([columns(own_ids, k, m) for m in range(blocks)], axis=1)
            mine = tok[0:rows, pl.ds(pl.multiple_of(s * depth, depth), depth)]
            theirs = tok[0:rows, pl.ds(pl.multiple_of(other * depth, depth), depth)]
            total = jnp.dot(mine, own, preferred_element_type=jnp.float32)
            return total + jnp.dot(theirs, wr[k], preferred_element_type=jnp.float32)

        for level in range(5):
            least = (8 >> level) if level < 4 else 0

            @pl.when((flips >= least) & (flips < max(2 * least, 1)))
            def _():
                total = partial()
                for before in range(level):
                    place = PLACE[before] + flips
                    for copy in halving(part, before, place):
                        copy.wait_recv()
                    here = 15 * part + place
                    total += code_in[here].astype(jnp.int32).astype(jnp.float32) * unit_in[here]
                if level == 4:
                    out_ref[0:rows, pl.ds(pl.multiple_of(part * wide, wide), wide)] = total.astype(out_ref.dtype)
                    return
                place = PLACE[level] + flips - least
                here = 15 * part + place
                most = jnp.maximum(jnp.max(jnp.abs(total), axis=0, keepdims=True), TINY)
                unit[here] = most * (1.0 / TOP)
                code[here] = jnp.round(total * (TOP / most)).astype(jnp.int32).astype(jnp.int16)
                for copy in halving(part, level, place):
                    copy.start()
        return carry

    lax.fori_loop(0, steps, run, 0)

    def drain(here, carry):
        part, place = lax.div(here, 15), lax.rem(here, 15)
        for copy in halving(part, 0, place):
            copy.wait_send()
        return carry

    lax.fori_loop(0, 15 * len(HALVING), drain, 0)


def plan(depth, ff, own_rows, block, T, n_blocks, live):
    sems = pltpu.SemaphoreType.DMA
    f32, bf16 = jnp.float32, jnp.bfloat16
    n = len(HALVING)
    wide = ff // (2 * T * n)
    shapes = [pltpu.SMEM((n_blocks,), jnp.int32), pltpu.VMEM((own_rows, 2 * T * depth), bf16)]
    shapes += [pltpu.VMEM((depth, ff), bf16), pltpu.VMEM((own_rows * T, 2 * depth), bf16)]
    shapes += [pltpu.VMEM((AHEAD, depth, wide), bf16), pltpu.VMEM((16 * n, depth, wide), bf16)]
    shapes += [pltpu.VMEM((15 * n, live, wide), jnp.int16), pltpu.VMEM((15 * n, 1, wide), f32)] * 2
    shapes += [pltpu.SMEM((16 * n * (wide // block),), jnp.int32)] * 2
    counts = ((), (), (), (T,), (T,), (AHEAD,), (16 * n,)) + ((15 * n,),) * 4
    return shapes + [sems(k) for k in counts]


def fits(depth, ff, own_rows, T, subs, n_blocks):
    n = len(HALVING)
    if T.bit_length() != 5 or T & (T - 1) or subs != 2 or n_blocks % (2 * T * n) or depth % (16 * LOADS) or own_rows % 16:
        return False
    rows, wide = own_rows * T, ff // (2 * T * n)
    used = 2 * (depth * ff + 2 * rows * 2 * depth + (AHEAD + 16 * n) * depth * wide + 30 * n * rows * wide)
    return used + 4 * rows * n * wide + (4 << 20) < VMEM_LIMIT


def on_device(stored, tokens, owner_map, live_count):
    depth, ff = stored.shape
    own_rows = tokens.shape[0]
    n_blocks = owner_map.shape[0]
    block = ff // n_blocks
    T, subs = lax.axis_size("tensor"), lax.axis_size("sub")
    if not fits(depth, ff, own_rows, T, subs, n_blocks):
        return portable(stored, tokens, owner_map, live_count)
    rows = own_rows * T
    unit = max(rows // 16, 16)
    sizes = [n for n in range(rows // 2, rows, unit)] + [rows]

    def call(n, which):
        run = pl.pallas_call(
            functools.partial(kernel, T, own_rows, block),
            out_shape=pltpu.VMEM((rows, ff // (2 * T)), jnp.bfloat16),
            in_specs=[pl.BlockSpec(memory_space=pl.ANY)] * 3,
            out_specs=pl.BlockSpec(memory_space=pltpu.VMEM),
            scratch_shapes=plan(depth, ff, own_rows, block, T, n_blocks, n),
            compiler_params=pltpu.CompilerParams(
                collective_id=which, has_side_effects=True, vmem_limit_bytes=VMEM_LIMIT),
        )

        def masked(live, *args):
            product = run(*args)
            across = product.shape[1]
            at = lax.broadcasted_iota(jnp.int32, product.shape, 0) * across + lax.broadcasted_iota(jnp.int32, product.shape, 1)
            keep = at < live * across
            return jnp.where(keep, product, jnp.bfloat16(0.0))

        return masked

    most = live_count[0]
    if lax.axis_size("groups") > 1:
        most = lax.pmax(most, "groups")
    which = sum((most > n).astype(jnp.int32) for n in sizes[:-1])
    return lax.switch(which, [call(n, i) for i, n in enumerate(sizes)], live_count[0], owner_map, tokens, stored)


def solution(mesh):
    placed = (P(("tensor", "sub"), None), P(("groups", "tensor"), None), P(), P("groups"))
    return jax.shard_map(
        on_device,
        mesh=mesh,
        in_specs=placed,
        out_specs=P("groups", ("tensor", "sub")),
        check_vma=False,
    )
```

```python
import functools

import jax
import jax.numpy as jnp
from jax import lax
from jax.experimental import pallas as pl
from jax.experimental.pallas import tpu as pltpu
from jax.sharding import PartitionSpec as P

MESH = pl.DeviceIdType.MESH
VMEM_LIMIT = 60 << 20
TOP = 32767.0
TINY = 1e-33
AHEAD = 4
LOADS = 8
HALVING = ((2, 0, 1, 3), (0, 2, 1, 3), (1, 0, 2, 3), (1, 0, 2, 3))
ORDER = (
    15, 43, 31, 29, 63, 13, 25, 47, 8, 27, 46, 14, 62, 23, 45, 7, 5, 9, 11, 61, 21, 39, 12, 30, 19, 10, 54, 59, 37, 26,
    41, 55, 6, 35, 44, 3, 17, 60, 40, 22, 28, 53, 57, 38, 33, 36, 51, 1, 42, 58, 18, 4, 20, 2, 49, 34, 24, 52, 50, 56, 0,
    32, 16, 48)
PLACE = (0, 8, 12, 14)


def portable(stored, tokens, owner_map, live_count):
    row_count = stored.shape[0]
    block_count = owner_map.shape[0]
    width = stored.shape[1] // block_count
    devices = lax.axis_size(("tensor", "sub"))
    per_dev = block_count // devices
    ordered = jnp.take(stored.reshape(row_count, block_count, width), owner_map, axis=1)
    gathered = lax.all_gather(tokens, "tensor", axis=0, tiled=True)
    sectioned = ordered.reshape(row_count, devices, per_dev, width)
    piece = lax.all_to_all(sectioned, ("tensor", "sub"), split_axis=1, concat_axis=0, tiled=True)
    weights = piece.reshape(piece.shape[0], piece.shape[2], piece.shape[3])
    result = jnp.einsum("td,dkc->tkc", gathered, weights, preferred_element_type=jnp.float32)
    product = result.reshape(result.shape[0], per_dev * width)
    row_ids = lax.broadcasted_iota(jnp.int32, (product.shape[0], 1), 0)
    keep = row_ids < live_count[0]
    return jnp.where(keep, product, jnp.float32(0.0)).astype(jnp.bfloat16)


def pick(values, at):
    if len(values) == 1:
        return values[0]
    half = len(values) // 2
    return jnp.where(at < half, pick(values[:half], at), pick(values[half:], at - half))


def lookup(k):
    words = [sum(v << (6 * j) for j, v in enumerate(ORDER[at:at + 4])) for at in range(0, len(ORDER), 4)]
    word = pick([jnp.int32(v) for v in words], lax.div(k, 4))
    return lax.rem(pick([lax.div(word, 64 ** j) for j in range(4)], lax.rem(k, 4)), 64)


def kernel(T, own_rows, block, live_hbm, map_hbm, tok_hbm, w_hbm, out_ref, live_ref, map_ref, tok_ref, w, tok, stage, wr, code, unit, code_in, unit_in,
           own_ids, other_ids, live_sem, map_sem, tok_sem, w_sem, ts, tr, ss, sr, cs, cr, fs, fr):
    t = lax.axis_index("tensor")
    s = lax.axis_index("sub")
    other = 1 - s
    depth = w.shape[0]
    rows, wide = code.shape[1:]
    blocks = wide // block
    per_dev = len(HALVING) * blocks
    steps = len(ORDER)
    bits = [lax.rem(t // 2 ** k, 2) for k in range(4)]
    far = [t + 2 ** k * (1 - 2 * bits[k]) for k in range(4)]

    barrier = pltpu.get_barrier_semaphore()
    for r in range(1, T):
        pl.semaphore_signal(barrier, inc=1, device_id={"tensor": lax.rem(t + r, T), "sub": s}, device_id_type=MESH)
    pl.semaphore_signal(barrier, inc=1, device_id={"tensor": t, "sub": other}, device_id_type=MESH)
    map_copy = pltpu.make_async_copy(map_hbm, map_ref, map_sem)
    map_copy.start()
    live_copy = pltpu.make_async_copy(live_hbm, live_ref, live_sem)
    live_copy.start()
    own_copy = pltpu.make_async_copy(tok_hbm, tok_ref, tok_sem)
    own_copy.start()
    own_copy.wait()
    span = depth // LOADS
    for c in range(LOADS):
        pltpu.make_async_copy(w_hbm.at[pl.ds(c * span, span), :], w.at[pl.ds(c * span, span), :], w_sem).start()
    pl.semaphore_wait(barrier, T)

    def token_copy(r):
        to = lax.rem(t + r, T)
        return pltpu.make_async_remote_copy(
            src_ref=tok_ref.at[:, pl.ds(pl.multiple_of(to * 2 * depth, 2 * depth), 2 * depth)],
            dst_ref=tok.at[pl.ds(pl.multiple_of(t * own_rows, own_rows), own_rows), :],
            send_sem=ts.at[r], recv_sem=tr.at[r],
            device_id={"tensor": to, "sub": s}, device_id_type=MESH)

    for r in range(1, T):
        token_copy(r).start()
    tok[pl.ds(pl.multiple_of(t * own_rows, own_rows), own_rows), :] = (
        tok_ref[:, pl.ds(pl.multiple_of(t * 2 * depth, 2 * depth), 2 * depth)])

    def sub_copy(k):
        slot = lax.rem(k, AHEAD)
        return pltpu.make_async_remote_copy(
            src_ref=stage.at[slot], dst_ref=wr.at[k], send_sem=ss.at[slot], recv_sem=sr.at[k],
            device_id={"tensor": t, "sub": other}, device_id_type=MESH)

    def halving(part, level, place):
        here = 15 * part + place
        to = {"tensor": pick([far[order[level]] for order in HALVING], part), "sub": s}
        return [
            pltpu.make_async_remote_copy(
                src_ref=unit.at[here], dst_ref=unit_in.at[here], send_sem=fs.at[here],
                recv_sem=fr.at[here], device_id=to, device_id_type=MESH),
            pltpu.make_async_remote_copy(
                src_ref=code.at[here], dst_ref=code_in.at[here], send_sem=cs.at[here],
                recv_sem=cr.at[here], device_id=to, device_id_type=MESH),
        ]

    map_copy.wait()
    live_copy.wait()
    moved = [0]
    for k in range(4):
        moved += [m + (far[k] - t) for m in moved]
    for k, step in enumerate(ORDER):
        part, flips = step // 16, step % 16
        which = sum(2 ** HALVING[part][j] for j in range(4) if flips >> (3 - j) & 1)
        for ids, sub in ((own_ids, s), (other_ids, other)):
            base = (2 * (t + moved[which]) + sub) * per_dev + part * blocks
            for m in range(blocks):
                ids[k * blocks + m] = map_ref[base + m]

    def columns(ids, k, m):
        return w[:, pl.ds(ids[k * blocks + m] * block, block)]

    def fill(k, at):
        for m in range(blocks):
            stage[lax.rem(k, AHEAD), :, m * block:(m + 1) * block] = columns(other_ids, at, m)

    pltpu.make_async_copy(w, w, w_sem).wait()
    for k in range(AHEAD):
        fill(k, k)
        sub_copy(k).start()
    for r in range(1, T):
        token_copy(r).wait()

    if rows < out_ref.shape[0]:
        out_ref[rows:, :] = jnp.zeros((out_ref.shape[0] - rows, out_ref.shape[1]), out_ref.dtype)

    def run(k, carry):
        step = lookup(k)
        part, flips = lax.div(step, 16), lax.rem(step, 16)
        sub_copy(k).wait()
        fill(k, jnp.minimum(k + AHEAD, steps - 1))

        @pl.when(k < steps - AHEAD)
        def _():
            sub_copy(k + AHEAD).start()

        def partial():
            own = jnp.concatenate([columns(own_ids, k, m) for m in range(blocks)], axis=1)
            mine = tok[0:rows, pl.ds(pl.multiple_of(s * depth, depth), depth)]
            theirs = tok[0:rows, pl.ds(pl.multiple_of(other * depth, depth), depth)]
            total = jnp.dot(mine, own, preferred_element_type=jnp.float32)
            return total + jnp.dot(theirs, wr[k], preferred_element_type=jnp.float32)

        for level in range(5):
            least = (8 >> level) if level < 4 else 0

            @pl.when((flips >= least) & (flips < max(2 * least, 1)))
            def _():
                total = partial()
                for before in range(level):
                    place = PLACE[before] + flips
                    for copy in halving(part, before, place):
                        copy.wait_recv()
                    here = 15 * part + place
                    total += code_in[here].astype(jnp.int32).astype(jnp.float32) * unit_in[here]
                if level == 4:
                    keep = lax.broadcasted_iota(jnp.int32, total.shape, 0) < live_ref[0]
                    total = jnp.where(keep, total, 0.0)
                    out_ref[0:rows, pl.ds(pl.multiple_of(part * wide, wide), wide)] = total.astype(out_ref.dtype)
                    return
                place = PLACE[level] + flips - least
                here = 15 * part + place
                most = jnp.maximum(jnp.max(jnp.abs(total), axis=0, keepdims=True), TINY)
                unit[here] = most * (1.0 / TOP)
                code[here] = jnp.round(total * (TOP / most)).astype(jnp.int32).astype(jnp.int16)
                for copy in halving(part, level, place):
                    copy.start()
        return carry

    lax.fori_loop(0, steps, run, 0)

    def drain(here, carry):
        part, place = lax.div(here, 15), lax.rem(here, 15)
        for copy in halving(part, 0, place):
            copy.wait_send()
        return carry

    lax.fori_loop(0, 15 * len(HALVING), drain, 0)


def plan(depth, ff, own_rows, block, T, n_blocks, live):
    sems = pltpu.SemaphoreType.DMA
    f32, bf16 = jnp.float32, jnp.bfloat16
    n = len(HALVING)
    wide = ff // (2 * T * n)
    shapes = [pltpu.SMEM((1,), jnp.int32), pltpu.SMEM((n_blocks,), jnp.int32), pltpu.VMEM((own_rows, 2 * T * depth), bf16)]
    shapes += [pltpu.VMEM((depth, ff), bf16), pltpu.VMEM((own_rows * T, 2 * depth), bf16)]
    shapes += [pltpu.VMEM((AHEAD, depth, wide), bf16), pltpu.VMEM((16 * n, depth, wide), bf16)]
    shapes += [pltpu.VMEM((15 * n, live, wide), jnp.int16), pltpu.VMEM((15 * n, 1, wide), f32)] * 2
    shapes += [pltpu.SMEM((16 * n * (wide // block),), jnp.int32)] * 2
    counts = ((), (), (), (), (T,), (T,), (AHEAD,), (16 * n,)) + ((15 * n,),) * 4
    return shapes + [sems(k) for k in counts]


def fits(depth, ff, own_rows, T, subs, n_blocks):
    n = len(HALVING)
    if T.bit_length() != 5 or T & (T - 1) or subs != 2 or n_blocks % (2 * T * n) or depth % (16 * LOADS) or own_rows % 16:
        return False
    rows, wide = own_rows * T, ff // (2 * T * n)
    used = 2 * (depth * ff + 2 * rows * 2 * depth + (AHEAD + 16 * n) * depth * wide + 30 * n * rows * wide)
    return used + 4 * rows * n * wide + (4 << 20) < VMEM_LIMIT


def on_device(stored, tokens, owner_map, live_count):
    depth, ff = stored.shape
    own_rows = tokens.shape[0]
    n_blocks = owner_map.shape[0]
    block = ff // n_blocks
    T, subs = lax.axis_size("tensor"), lax.axis_size("sub")
    if not fits(depth, ff, own_rows, T, subs, n_blocks):
        return portable(stored, tokens, owner_map, live_count)
    rows = own_rows * T
    unit = max(rows // 16, 16)
    sizes = [n for n in range(rows // 2, rows, unit)] + [rows]

    def call(n, which):
        return pl.pallas_call(
            functools.partial(kernel, T, own_rows, block),
            out_shape=pltpu.VMEM((rows, ff // (2 * T)), jnp.bfloat16),
            in_specs=[pl.BlockSpec(memory_space=pl.ANY)] * 4,
            out_specs=pl.BlockSpec(memory_space=pltpu.VMEM),
            scratch_shapes=plan(depth, ff, own_rows, block, T, n_blocks, n),
            compiler_params=pltpu.CompilerParams(
                collective_id=which, has_side_effects=True, vmem_limit_bytes=VMEM_LIMIT),
        )

    most = live_count[0]
    if lax.axis_size("groups") > 1:
        most = lax.pmax(most, "groups")
    which = sum((most > n).astype(jnp.int32) for n in sizes[:-1])
    return lax.switch(which, [call(n, i) for i, n in enumerate(sizes)], live_count, owner_map, tokens, stored)


def solution(mesh):
    placed = (P(("tensor", "sub"), None), P(("groups", "tensor"), None), P(), P("groups"))
    return jax.shard_map(
        on_device,
        mesh=mesh,
        in_specs=placed,
        out_specs=P("groups", ("tensor", "sub")),
        check_vma=False,
    )
```
